32 devices in a mesh: row: 2 (over x), col: 4 (over z), freq: 4 (over y, core).
Axes of the slice: x: 2, y: 2, z: 4, core: 2. Of those that a mesh axis runs over, the one named last changes fastest.
Arguments:
- data: bfloat16 [2, 4, 2048, 2048], P(None, 'freq', 'row', 'col'), may hold values from -4.7729708 to 4.7729708, as said below
- primaries: bfloat16 [2, 4, 2048, 2048], P(None, 'freq', 'row', 'col'), may hold values from -6 to 6
Outputs:
- updated_primaries: bfloat16 [2, 4, 2048, 2048], P(None, 'freq', 'row', 'col')
- updated_residual: float32 [2, 4, 2048, 2048], P(None, 'freq', 'row', 'col')
The draws below stay inside these ranges and needn't reach their ends.
Inputs may be any that keep to these rules, and one draw needn't show every extreme that they name: `data`: magnitudes vary by source, receiver and frequency.
All inputs are finite; a program needn't handle non-finite values.
Results may differ from the reference program's by a relative error of at most 0.0045.
Values may be sent and summed in bfloat16 or wider, within the bound.
No kernel may reach another device: no remote copies, remote signals or barrier semaphores. Data moves between devices by JAX's collectives and lax.ppermute only.
A program may use at most 128 MiB of HBM per device.

```python
import math
import jax
import jax.numpy as jnp

N = 2048
NF = 4


def draw_data(key, part):
    base_key, row_key, col_key = jax.random.split(jax.random.fold_in(key, 17), 3)
    base = jnp.clip(jax.random.normal(base_key, (2, NF, N, N), jnp.float32), -4.0, 4.0)
    ramp = jnp.exp(math.log(3.0) * jnp.arange(N, dtype=jnp.float32) / (N - 1))
    row_scale = ramp * jax.random.uniform(row_key, (N,), jnp.float32, 0.5, 2.0)
    col_scale = ramp * jax.random.uniform(col_key, (N,), jnp.float32, 0.5, 2.0)
    freq_scale = jnp.exp(math.log(3.0) * jnp.arange(NF, dtype=jnp.float32) / max(NF - 1, 1))
    scaled = base * row_scale[None, None, :, None] * col_scale[None, None, None, :] * freq_scale[None, :, None, None]
    scaled = scaled / (2.0 * math.sqrt(N))
    return scaled.astype(jnp.bfloat16)


def block_levels(key, shape, pieces, smallest, high):
    level = 1.0
    for position, shards_of in pieces:
        heights = jax.random.uniform(jax.random.fold_in(jax.random.fold_in(key, 6), position), (shards_of,), jnp.float32, smallest / len(pieces), high / len(pieces))
        level = level * jnp.repeat(jnp.exp(heights), shape[position] // shards_of).reshape((-1,) + (1,) * (len(shape) - 1 - position))
    return level


def centred(own_key, shape, spread, most, pieces=(), kind=jnp.bfloat16):
    gain = block_levels(own_key, shape, pieces, -0.22, 0.18) if pieces else 1.0
    values = jax.random.normal(own_key, shape, jnp.float32) * spread * gain
    return jnp.minimum(jnp.maximum(values, -most), most).astype(kind)


def setup_inputs(seed: int = 0) -> dict:
    keys = jax.random.split(jax.random.key(seed), 3)
    return {
        "data": draw_data(jax.random.fold_in(keys[2], 71), 0),
        "primaries": centred(keys[1], (2, NF, N, N), 1.0, 6.0, ((1, 4), (2, 2), (3, 4))),
    }


def complex_product(a_re, a_im, b_re, b_im):
    real = jnp.dot(a_re, b_re, preferred_element_type=jnp.float32) - jnp.dot(a_im, b_im, preferred_element_type=jnp.float32)
    imag = jnp.dot(a_re, b_im, preferred_element_type=jnp.float32) + jnp.dot(a_im, b_re, preferred_element_type=jnp.float32)
    return real, imag


def one_frequency(data_f, prim_f):
    fwd_re, fwd_im = complex_product(prim_f[0], prim_f[1], data_f[0], data_f[1])
    res_re = data_f[0].astype(jnp.float32) - prim_f[0].astype(jnp.float32) + fwd_re
    res_im = data_f[1].astype(jnp.float32) - prim_f[1].astype(jnp.float32) + fwd_im
    rb_re = res_re.astype(jnp.bfloat16)
    rb_im = res_im.astype(jnp.bfloat16)
    adj_re, adj_im = complex_product(rb_re, rb_im, data_f[0].T, (-data_f[1]).T)
    grad_re = (adj_re - res_re).astype(jnp.bfloat16)
    grad_im = (adj_im - res_im).astype(jnp.bfloat16)
    gp_re, gp_im = complex_product(grad_re, grad_im, data_f[0], data_f[1])
    chg_re = gp_re - grad_re.astype(jnp.float32)
    chg_im = gp_im - grad_im.astype(jnp.float32)
    return (jnp.stack([res_re, res_im]), jnp.stack([grad_re, grad_im]), jnp.stack([chg_re, chg_im]))


def reference(data, primaries):
    residuals = []
    gradients = []
    changes = []
    for freq_index in range(NF):
        res, grad, chg = one_frequency(data[:, freq_index], primaries[:, freq_index])
        residuals.append(res)
        gradients.append(grad)
        changes.append(chg)
    residual = jnp.stack(residuals, axis=1)
    gradient = jnp.stack(gradients, axis=1)
    change = jnp.stack(changes, axis=1)
    inner = jnp.sum(change * residual)
    energy = jnp.sum(change * change) + 1e-6
    step = -inner / energy
    updated_primaries = (primaries.astype(jnp.float32) + step * gradient.astype(jnp.float32)).astype(jnp.bfloat16)
    updated_residual = residual + step * change
    return updated_primaries, updated_residual
```

```python
import jax
import jax.numpy as jnp
from jax import lax
from jax.experimental import pallas as pl
from jax.experimental.pallas import tpu as pltpu
from jax.sharding import PartitionSpec as P

VMEM_BYTES = 56 * 1024 * 1024
MESSAGE_GROUPS = ((0, 1), (2, 3))


def batched(left, right):
    return jnp.einsum("fik,fkj->fij", left, right, preferred_element_type=jnp.float32)


def complex_product(left, right):
    real = batched(left[0], right[0]) - batched(left[1], right[1])
    imag = batched(left[0], right[1]) + batched(left[1], right[0])
    return jnp.stack([real, imag])


def blocked_gradient(data_part, primary_part):
    src_rows = data_part.shape[2]
    columns = lax.all_gather(data_part, "row", axis=2, tiled=True)

    def add_block(piece):
        return complex_product(piece, columns)

    forward = add_block(lax.all_gather(primary_part, "col", axis=3, tiled=True))
    residual = data_part.astype(jnp.float32) - primary_part.astype(jnp.float32) + forward
    rounded = residual.astype(jnp.bfloat16)
    real = jnp.einsum("fjk,fik->jfi", columns[0], rounded[0], preferred_element_type=jnp.float32)
    real = real + jnp.einsum(
        "fjk,fik->jfi", columns[1], rounded[1], preferred_element_type=jnp.float32
    )
    imag = jnp.einsum("fjk,fik->jfi", columns[0], rounded[1], preferred_element_type=jnp.float32)
    imag = imag - jnp.einsum(
        "fjk,fik->jfi", columns[1], rounded[0], preferred_element_type=jnp.float32
    )
    summed = lax.psum_scatter(
        jnp.concatenate([real, imag], axis=2), "col", scatter_dimension=0, tiled=True
    )
    adjoint = jnp.stack([summed[:, :, :src_rows], summed[:, :, src_rows:]]).transpose(0, 2, 3, 1)
    gradient = (adjoint - residual).astype(jnp.bfloat16)
    moved = add_block(lax.all_gather(gradient, "col", axis=3, tiled=True))
    change = moved - gradient.astype(jnp.float32)
    return (residual, gradient, change)


def blocked(data, primaries):
    res, grad, chg = blocked_gradient(data, primaries)
    inner_local = jnp.sum(chg * res)
    energy_local = jnp.sum(chg * chg)
    inner, energy = lax.psum((inner_local, energy_local), ("row", "col", "freq"))
    step = -inner / (energy + 1e-06)
    updated_primaries = (primaries.astype(jnp.float32) + step * grad.astype(jnp.float32)).astype(
        jnp.bfloat16
    )
    updated_residual = res + step * chg
    return (updated_primaries, updated_residual)


class Plan:
    def __init__(self, rows, cols, freqs):
        self.rows, self.cols, self.freqs = rows, cols, freqs

    def send(self, k):
        pairs = []
        for z in range(self.cols):
            for f in range(self.freqs):
                part, half = z ^ k, f % 2
                home = half * self.cols // 2 + part // 2
                pairs.append((z * self.freqs + f, home * self.freqs + f // 2 * 2 + part % 2))
        return pairs

    def to_home(self, blocks, z, k):
        piece = lax.dynamic_index_in_dim(blocks, z ^ k, 1, keepdims=False)
        return lax.ppermute(piece, ("col", "freq"), self.send(k))

    def from_home(self, piece, k):
        return lax.ppermute(piece, ("col", "freq"), [(b, a) for a, b in self.send(k)])

    def over_row(self, value):
        return lax.ppermute(value, "row", [(i, i ^ 1) for i in range(self.rows)])

    def over_core(self, value):
        return lax.ppermute(value, "freq", [(i, i ^ 1) for i in range(self.freqs)])

    def over_freq(self, value):
        return lax.ppermute(value, "freq", [(i, i ^ 2) for i in range(self.freqs)])

    def over_col(self, value, by):
        return lax.ppermute(value, "col", [(i, i ^ by) for i in range(self.cols)])

    def total(self, value):
        value = value + self.over_core(value)
        value = value + self.over_col(value, 1)
        value = value + self.over_col(value, 2)
        value = value + self.over_row(value)
        return value + self.over_freq(value)


def place_copies(where, buffers, slots, data_v, sems, rows):
    row_index, part = where
    copies = {}
    for number, (slot, (dx, dp, k)) in enumerate(slots):
        ref, sub = buffers[slot[0]], slot[1]
        start = ((row_index ^ dx) * 4 + (part ^ dp)) * rows
        target = data_v.at[dp ^ k, :, pl.ds(pl.multiple_of(start, rows), rows), :]
        source = ref if sub is None else ref.at[sub]
        copies.setdefault(dp ^ k, []).append(pltpu.make_async_copy(source, target, sems.at[number]))
    return copies


def product(stacked, right, rows):
    one = jnp.dot(stacked, right[0], preferred_element_type=jnp.float32)
    two = jnp.dot(stacked, right[1], preferred_element_type=jnp.float32)
    return one[:rows] - two[rows:], one[rows:] + two[:rows]


def residual_gradient_kernel(slots, n_buffers, rows, width, where_ref, *refs):
    buffers, refs = refs[:n_buffers], refs[n_buffers:]
    x_refs, refs = refs[:4], refs[4:]
    r_out, refs = refs[0], refs[1:]
    g_outs, refs = refs[:4], refs[4:]
    data_v, rows_v, x_v, r_v, rb_v, g_v, sems, x_sems, out_sems = refs
    row_index, part = where_ref[0], where_ref[1]
    copies = place_copies((row_index, part), buffers, slots, data_v, sems, rows)
    x_copies = []
    for k in range(4):
        at = pl.ds(pl.multiple_of((part ^ k) * width, width), width)
        for i in range(2):
            x_copies.append(
                pltpu.make_async_copy(
                    x_refs[k].at[i], rows_v.at[pl.ds(i * rows, rows), at], x_sems.at[3 * k + i]
                )
            )
        x_copies.append(pltpu.make_async_copy(x_refs[k], x_v.at[k], x_sems.at[3 * k + 2]))
    for copy in x_copies:
        copy.start()
    for t in range(4):
        for copy in copies[t]:
            copy.start()
    for copy in x_copies:
        copy.wait()
    own = pl.ds(pl.multiple_of((row_index * 4 + part) * rows, rows), rows)
    outs = []
    for t in range(4):
        for copy in copies[t]:
            copy.wait()
        forward = product(rows_v[...], (data_v[t, 0], data_v[t, 1]), rows)
        for i in range(2):
            residual = (
                data_v[t, i, own, :].astype(jnp.float32)
                - x_v[t, i].astype(jnp.float32)
                + forward[i]
            )
            r_v[t, i] = residual
            rb_v[t, i * rows : (i + 1) * rows, :] = residual.astype(jnp.bfloat16)
        copy = pltpu.make_async_copy(r_v.at[t], r_out.at[t], out_sems.at[t])
        copy.start()
        outs.append(copy)

    def against(left, right):
        return lax.dot_general(
            left, right, (((1,), (1,)), ((), ())), preferred_element_type=jnp.float32
        )

    for k in range(4):
        at = pl.ds(pl.multiple_of((part ^ k) * width, width), width)
        one = against(rb_v[0], data_v[0, 0, at, :])
        two = against(rb_v[0], data_v[0, 1, at, :])
        for t in range(1, 4):
            one = one + against(rb_v[t], data_v[t, 0, at, :])
            two = two + against(rb_v[t], data_v[t, 1, at, :])
        g_v[k, 0] = (one[:rows] + two[rows:] - r_v[k, 0]).astype(jnp.bfloat16)
        g_v[k, 1] = (one[rows:] - two[:rows] - r_v[k, 1]).astype(jnp.bfloat16)
        copy = pltpu.make_async_copy(g_v.at[k], g_outs[k], out_sems.at[4 + k])
        copy.start()
        outs.append(copy)
    for copy in outs:
        copy.wait()


def change_kernel(slots, n_buffers, rows, width, where_ref, *refs):
    buffers, refs = refs[:n_buffers], refs[n_buffers:]
    g_refs, refs = refs[:4], refs[4:]
    r_in, c_out, sums_out, refs = refs[0], refs[1], refs[2], refs[3:]
    data_v, rows_v, g_v, r_v, c_v, sems, g_sems, r_sems, out_sems = refs
    row_index, part = where_ref[0], where_ref[1]
    copies = place_copies((row_index, part), buffers, slots, data_v, sems, rows)
    g_copies = []
    for k in range(4):
        at = pl.ds(pl.multiple_of((part ^ k) * width, width), width)
        for i in range(2):
            g_copies.append(
                pltpu.make_async_copy(
                    g_refs[k].at[i], rows_v.at[pl.ds(i * rows, rows), at], g_sems.at[3 * k + i]
                )
            )
        g_copies.append(pltpu.make_async_copy(g_refs[k], g_v.at[k], g_sems.at[3 * k + 2]))
    for copy in g_copies:
        copy.start()
    r_copies = []
    for t in range(4):
        for copy in copies[t]:
            copy.start()
        r_copies.append(pltpu.make_async_copy(r_in.at[t], r_v.at[t], r_sems.at[t]))
        r_copies[t].start()
    for copy in g_copies:
        copy.wait()
    inner = jnp.float32(0)
    energy = jnp.float32(0)
    outs = []
    for t in range(4):
        for copy in copies[t]:
            copy.wait()
        moved = product(rows_v[...], (data_v[t, 0], data_v[t, 1]), rows)
        r_copies[t].wait()
        for i in range(2):
            change = moved[i] - g_v[t, i].astype(jnp.float32)
            c_v[t, i] = change
            inner = inner + jnp.sum(change * r_v[t, i])
            energy = energy + jnp.sum(change * change)
        copy = pltpu.make_async_copy(c_v.at[t], c_out.at[t], out_sems.at[t])
        copy.start()
        outs.append(copy)
    sums_out[0] = inner
    sums_out[1] = energy
    for copy in outs:
        copy.wait()


def whole_rows(plan, data, primaries):
    z = lax.axis_index("col")
    row_index = lax.axis_index("row")
    part = z % (plan.cols // 2) * 2 + lax.axis_index("freq") % 2
    n_rows, width = data.shape[2], data.shape[3]
    rows = n_rows // plan.cols
    where = jnp.stack([row_index, part]).astype(jnp.int32)
    data_blocks = data.reshape(2, plan.cols, rows, width)
    prim_blocks = primaries.reshape(2, plan.cols, rows, width)

    buffers, slots = [], []
    arrived = None
    for group in MESSAGE_GROUPS:
        own = [plan.to_home(data_blocks, z, k) for k in group]
        arrived = own
        own = own[0] if len(group) == 1 else jnp.stack(own)
        held = {(0, 0): own}
        held[(0, 2)] = plan.over_col(own, 1)
        held.update({(1, dp): plan.over_row(v) for (_, dp), v in list(held.items())})
        held.update({(dx, dp ^ 1): plan.over_core(v) for (dx, dp), v in list(held.items())})
        for (dx, dp), value in held.items():
            for sub, k in enumerate(group):
                slots.append(((len(buffers), None if len(group) == 1 else sub), (dx, dp, k)))
            buffers.append(value)

    later, _ = lax.optimization_barrier((prim_blocks, arrived))
    x_parts = [plan.to_home(later, z, k) for k in range(4)]

    hbm = pl.BlockSpec(memory_space=pl.ANY)
    smem = pl.BlockSpec(memory_space=pltpu.SMEM)
    message = jax.ShapeDtypeStruct((2, rows, width), jnp.bfloat16)
    wide = jax.ShapeDtypeStruct((4, 2, rows, width), jnp.float32)
    params = pltpu.CompilerParams(vmem_limit_bytes=VMEM_BYTES)
    n_buffers = len(buffers)
    data_scratch = pltpu.VMEM((4, 2, 8 * rows, width), jnp.bfloat16)
    sems = pltpu.SemaphoreType.DMA((len(slots),))

    def first(*refs):
        residual_gradient_kernel(slots, n_buffers, rows, width, *refs)

    residual, *gradient = pl.pallas_call(
        first,
        in_specs=[smem] + [hbm] * (n_buffers + 4),
        out_specs=[hbm] * 5,
        out_shape=[wide] + [message] * 4,
        scratch_shapes=[
            data_scratch,
            pltpu.VMEM((2 * rows, 4 * width), jnp.bfloat16),
            pltpu.VMEM((4, 2, rows, width), jnp.bfloat16),
            pltpu.VMEM((4, 2, rows, width), jnp.float32),
            pltpu.VMEM((4, 2 * rows, width), jnp.bfloat16),
            pltpu.VMEM((4, 2, rows, width), jnp.bfloat16),
            sems,
            pltpu.SemaphoreType.DMA((12,)),
            pltpu.SemaphoreType.DMA((8,)),
        ],
        compiler_params=params,
        name="residual_gradient",
    )(where, *buffers, *x_parts)

    returned = [plan.from_home(gradient[k], k) for k in range(4)]

    def second(*refs):
        change_kernel(slots, n_buffers, rows, width, *refs)

    change, sums = pl.pallas_call(
        second,
        in_specs=[smem] + [hbm] * (n_buffers + 5),
        out_specs=[hbm, smem],
        out_shape=[wide, jax.ShapeDtypeStruct((2,), jnp.float32)],
        scratch_shapes=[
            data_scratch,
            pltpu.VMEM((2 * rows, 4 * width), jnp.bfloat16),
            pltpu.VMEM((4, 2, rows, width), jnp.bfloat16),
            pltpu.VMEM((4, 2, rows, width), jnp.float32),
            pltpu.VMEM((4, 2, rows, width), jnp.float32),
            sems,
            pltpu.SemaphoreType.DMA((12,)),
            pltpu.SemaphoreType.DMA((4,)),
            pltpu.SemaphoreType.DMA((4,)),
        ],
        compiler_params=params,
        name="change",
    )(where, *buffers, *gradient, residual)

    sums = plan.total(sums)
    step = -sums[0] / (sums[1] + 1e-06)

    new_primaries = jnp.zeros((2, plan.cols, rows, width), jnp.bfloat16)
    new_residual = jnp.zeros((2, plan.cols, rows, width), jnp.float32)
    updated = [(residual[k] + step * change[k]).astype(jnp.bfloat16) for k in range(4)]
    updated = [plan.from_home(updated[k], k) for k in range(4)]
    for k in range(4):
        old = lax.dynamic_index_in_dim(prim_blocks, z ^ k, 1, keepdims=False)
        new = old.astype(jnp.float32) + step * returned[k].astype(jnp.float32)
        new_primaries = lax.dynamic_update_index_in_dim(
            new_primaries, new.astype(jnp.bfloat16), z ^ k, 1
        )
        new_residual = lax.dynamic_update_index_in_dim(
            new_residual, updated[k].astype(jnp.float32), z ^ k, 1
        )
    return new_primaries.reshape(data.shape), new_residual.reshape(data.shape)


def solution(mesh):
    rows, cols, freqs = (mesh.shape[name] for name in ("row", "col", "freq"))

    def local(data, primaries):
        if (rows, cols, freqs) == (2, 4, 4):
            return whole_rows(Plan(rows, cols, freqs), data, primaries)
        return blocked(data, primaries)

    spec = P(None, "freq", "row", "col")
    return jax.shard_map(
        local, mesh=mesh, in_specs=(spec, spec), out_specs=(spec, spec), check_vma=False
    )
```

```python
import jax
import jax.numpy as jnp
import numpy as np
from jax import lax
from jax.experimental import pallas as pl
from jax.experimental.pallas import tpu as pltpu
from jax.sharding import Mesh
from jax.sharding import PartitionSpec as P

VMEM_BYTES = 16 * 1024 * 1024


def batched(left, right):
    return jnp.einsum("fik,fkj->fij", left, right, preferred_element_type=jnp.float32)


def complex_product(left, right):
    real = batched(left[0], right[0]) - batched(left[1], right[1])
    imag = batched(left[0], right[1]) + batched(left[1], right[0])
    return jnp.stack([real, imag])


def blocked_gradient(data_part, primary_part):
    src_rows = data_part.shape[2]
    columns = lax.all_gather(data_part, "row", axis=2, tiled=True)

    def add_block(piece):
        return complex_product(piece, columns)

    forward = add_block(lax.all_gather(primary_part, "col", axis=3, tiled=True))
    residual = data_part.astype(jnp.float32) - primary_part.astype(jnp.float32) + forward
    rounded = residual.astype(jnp.bfloat16)
    real = jnp.einsum("fjk,fik->jfi", columns[0], rounded[0], preferred_element_type=jnp.float32)
    real = real + jnp.einsum(
        "fjk,fik->jfi", columns[1], rounded[1], preferred_element_type=jnp.float32
    )
    imag = jnp.einsum("fjk,fik->jfi", columns[0], rounded[1], preferred_element_type=jnp.float32)
    imag = imag - jnp.einsum(
        "fjk,fik->jfi", columns[1], rounded[0], preferred_element_type=jnp.float32
    )
    summed = lax.psum_scatter(
        jnp.concatenate([real, imag], axis=2), "col", scatter_dimension=0, tiled=True
    )
    adjoint = jnp.stack([summed[:, :, :src_rows], summed[:, :, src_rows:]]).transpose(0, 2, 3, 1)
    gradient = (adjoint - residual).astype(jnp.bfloat16)
    moved = add_block(lax.all_gather(gradient, "col", axis=3, tiled=True))
    change = moved - gradient.astype(jnp.float32)
    return (residual, gradient, change)


def blocked(data, primaries):
    res, grad, chg = blocked_gradient(data, primaries)
    inner_local = jnp.sum(chg * res)
    energy_local = jnp.sum(chg * chg)
    inner, energy = lax.psum((inner_local, energy_local), ("row", "col", "freq"))
    step = -inner / (energy + 1e-06)
    updated_primaries = (primaries.astype(jnp.float32) + step * grad.astype(jnp.float32)).astype(
        jnp.bfloat16
    )
    updated_residual = res + step * chg
    return (updated_primaries, updated_residual)


FINE = ("row", "half", "pair", "twin", "lane")
HOME = ("row", "pair", "lane")
MESSAGES = 4
GROUPS = ((0, 1), (2, 3))


def send_pairs(k):
    pairs = []
    for z in range(4):
        for f in range(4):
            twin, lane, part = f // 2, f % 2, z ^ k
            pairs.append((z * 4 + f, (lane * 2 + part // 2) * 4 + twin * 2 + part % 2))
    return pairs


COLUMN = ("half", "pair", "twin", "lane")


def to_home(blocks, z, k):
    piece = lax.dynamic_index_in_dim(blocks, z ^ k, 1, keepdims=False)
    return lax.ppermute(piece, COLUMN, send_pairs(k))


def from_home(piece, k):
    return lax.ppermute(piece, COLUMN, [(b, a) for a, b in send_pairs(k)])


def total(value):
    swap = [(0, 1), (1, 0)]
    for axis in ("lane", "pair", "half", "row", "twin"):
        value = value + lax.ppermute(value, axis, swap)
    return value


def place_copies(group, buffer, data_v, sems, rows):
    copies = [[] for _ in range(4)]
    number = 0
    for device in range(8):
        for sub, k in enumerate(group):
            row_index, part = device // 4, device % 4
            at = pl.ds((row_index * 2 + part % 2) * rows, rows)
            target = data_v.at[part ^ k, :, at, :]
            copies[part ^ k].append(
                pltpu.make_async_copy(buffer.at[device, sub], target, sems.at[number])
            )
            number += 1
    return copies


def column_place(z):
    return z % 2 * 2 + z // 2


def message_copies(refs, part, wide_v, sems, rows, width):
    copies = []
    for k in range(4):
        start = pl.multiple_of(column_place(part ^ k) * width, width)
        for i in range(2):
            target = wide_v.at[pl.ds(i * rows, rows), pl.ds(start, width)]
            copies.append(pltpu.make_async_copy(refs[k].at[i], target, sems.at[2 * k + i]))
    return copies


def product(stacked, right, n, rows):
    one = jnp.dot(stacked, right[n, 0], preferred_element_type=jnp.float32)
    two = jnp.dot(stacked, right[n, 1], preferred_element_type=jnp.float32)
    return one[:rows] - two[rows:], one[rows:] + two[:rows]


def columns_of(wide_v, pair, width):
    return wide_v[:, pair * 2 * width : (pair + 1) * 2 * width]


def against(left, right):
    dims = (((1,), (1,)), ((), ()))
    return lax.dot_general(left, right, dims, preferred_element_type=jnp.float32)


def gradient_blocks(second, part, a_v, b_v, r_v, rb_v, g_v, g_outs, sems, rows, width):
    half = part // 2
    if second:
        half = 1 - half
    at = pl.ds(pl.multiple_of(half * width, width), width)
    for odd in range(2):
        one = two = None
        for n in range(4):
            source = a_v if odd == n // 2 else b_v
            first_dot = against(rb_v[n], source[n, 0, at, :])
            second_dot = against(rb_v[n], source[n, 1, at, :])
            one = first_dot if one is None else one + first_dot
            two = second_dot if two is None else two + second_dot
        slot = part % 2 ^ odd
        k = slot + 2 * second
        g_v[slot, 0] = (one[:rows] + two[rows:] - r_v[k, 0]).astype(jnp.bfloat16)
        g_v[slot, 1] = (one[rows:] - two[:rows] - r_v[k, 1]).astype(jnp.bfloat16)
    outs = [pltpu.make_async_copy(g_v.at[j], g_outs[j], sems.at[j]) for j in range(2)]
    for copy in outs:
        copy.start()
    for copy in outs:
        copy.wait()


def forward_kernel(rows, width, where_ref, a_in, *refs):
    x_refs, (a_v, wide_v, f_v, sems, x_sems) = refs[:4], refs[4:]
    copies = place_copies(GROUPS[0], a_in, a_v, sems, rows)
    x_copies = message_copies(x_refs, where_ref[1], wide_v, x_sems, rows, width)
    for copy in copies[0] + x_copies + copies[1]:
        copy.start()
    for copy in x_copies:
        copy.wait()
    for n in range(4):
        for copy in copies[n]:
            copy.wait()
        if n < 2:
            for copy in copies[n + 2]:
                copy.start()
        forward = product(columns_of(wide_v, n // 2, width), a_v, n, rows)
        for i in range(2):
            f_v[n, i] = forward[i]


def residual_kernel(rows, width, where_ref, b_in, a_v, wide_v, f_v, *refs):
    b_v, r_v, rb_v, g0, g1, g_v, sems, out_sems = refs
    row_index, part = where_ref[0], where_ref[1]
    copies = place_copies(GROUPS[1], b_in, b_v, sems, rows)
    for copy in copies[0] + copies[1]:
        copy.start()
    own = pl.ds(pl.multiple_of((row_index * 2 + part % 2) * rows, rows), rows)
    for n in range(4):
        for copy in copies[n]:
            copy.wait()
        if n < 2:
            for copy in copies[n + 2]:
                copy.start()
        forward = product(columns_of(wide_v, 1 - n // 2, width), b_v, n, rows)
        place = column_place(n) * width
        for i in range(2):
            data = jnp.where(
                part // 2 == n // 2,
                a_v[n, i, own, :].astype(jnp.float32),
                b_v[n, i, own, :].astype(jnp.float32),
            )
            x = wide_v[i * rows : (i + 1) * rows, place : place + width].astype(jnp.float32)
            residual = data - x + (f_v[n, i] + forward[i])
            r_v[part ^ n, i] = residual
            rb_v[n, i * rows : (i + 1) * rows, :] = residual.astype(jnp.bfloat16)
    gradient_blocks(0, part, a_v, b_v, r_v, rb_v, g_v, (g0, g1), out_sems, rows, width)


def gradient_kernel(rows, width, where_ref, a_v, b_v, r_v, rb_v, g2, g3, g_v, out_sems):
    part = where_ref[1]
    gradient_blocks(1, part, a_v, b_v, r_v, rb_v, g_v, (g2, g3), out_sems, rows, width)


def change_kernel(rows, width, where_ref, a_v, b_v, r_v, *refs):
    g_refs, (c_v, sums_out, wide_v, g_sems) = refs[:4], refs[4:]
    part = where_ref[1]
    g_copies = message_copies(g_refs, part, wide_v, g_sems, rows, width)
    for copy in g_copies:
        copy.start()
    for copy in g_copies:
        copy.wait()
    inner = jnp.zeros((rows, width), jnp.float32)
    energy = jnp.zeros((rows, width), jnp.float32)
    for n in range(4):
        from_a = product(columns_of(wide_v, n // 2, width), a_v, n, rows)
        from_b = product(columns_of(wide_v, 1 - n // 2, width), b_v, n, rows)
        place = column_place(n) * width
        for i in range(2):
            g = wide_v[i * rows : (i + 1) * rows, place : place + width].astype(jnp.float32)
            change = from_a[i] + from_b[i] - g
            c_v[part ^ n, i] = change
            inner = inner + change * r_v[part ^ n, i]
            energy = energy + change * change
    sums_out[0] = jnp.sum(inner)
    sums_out[1] = jnp.sum(energy)


def whole_rows(data, primaries):
    z = lax.axis_index("half") * 2 + lax.axis_index("pair")
    part = lax.axis_index("pair") * 2 + lax.axis_index("lane")
    n_rows, width = data.shape[2], data.shape[3]
    rows = n_rows // MESSAGES
    where = jnp.stack([lax.axis_index("row"), part]).astype(jnp.int32)
    data_blocks = data.reshape(2, MESSAGES, rows, width)
    prim_blocks = primaries.reshape(2, MESSAGES, rows, width)

    arrived = [to_home(data_blocks, z, k) for k in range(MESSAGES)]
    buffers = []
    for group in GROUPS:
        own = jnp.stack([arrived[k] for k in group])
        buffers.append(lax.all_gather(own, HOME))
    later, _ = lax.optimization_barrier((prim_blocks, arrived[1]))
    x_parts = [to_home(later, z, k) for k in range(MESSAGES)]

    hbm = pl.BlockSpec(memory_space=pl.ANY)
    vmem = pl.BlockSpec(memory_space=pltpu.VMEM)
    smem = pl.BlockSpec(memory_space=pltpu.SMEM)
    message = jax.ShapeDtypeStruct((2, rows, width), jnp.bfloat16)
    f32_blocks = pltpu.VMEM((4, 2, rows, width), jnp.float32)
    data_half = pltpu.VMEM((4, 2, 4 * rows, width), jnp.bfloat16)
    wide = pltpu.VMEM((2 * rows, 4 * width), jnp.bfloat16)
    rounded = pltpu.VMEM((4, 2 * rows, width), jnp.bfloat16)
    two_messages = pltpu.VMEM((2, 2, rows, width), jnp.bfloat16)
    dma = pltpu.SemaphoreType.DMA
    one_product = 8 * rows * (4 * width) * (4 * width)

    def call(kernel, name, products, in_specs, out_specs, out_shape, scratch):
        return pl.pallas_call(
            lambda *refs: kernel(rows, width, *refs),
            in_specs=[smem] + in_specs,
            out_specs=out_specs,
            out_shape=out_shape,
            scratch_shapes=scratch,
            compiler_params=pltpu.CompilerParams(vmem_limit_bytes=VMEM_BYTES),
            cost_estimate=pl.CostEstimate(
                flops=int(products * one_product), transcendentals=0, bytes_accessed=1 << 24
            ),
            name=name,
        )

    data_a, x_wide, partial = call(
        forward_kernel,
        "forward",
        0.5,
        [hbm] * 5,
        [vmem] * 3,
        [data_half, wide, f32_blocks],
        [dma((16,)), dma((8,))],
    )(where, buffers[0], *x_parts)
    data_b, residual, res_rounded, g0, g1 = call(
        residual_kernel,
        "residual",
        1.0,
        [hbm] + [vmem] * 3,
        [vmem] * 3 + [hbm] * 2,
        [data_half, f32_blocks, rounded, message, message],
        [two_messages, dma((16,)), dma((2,))],
    )(where, buffers[1], data_a, x_wide, partial)
    g2, g3 = call(
        gradient_kernel,
        "gradient",
        0.5,
        [vmem] * 4,
        [hbm] * 2,
        [message, message],
        [two_messages, dma((2,))],
    )(where, data_a, data_b, residual, res_rounded)
    gradient = [g0, g1, g2, g3]
    returned = [from_home(gradient[k], k) for k in range(4)]
    change, sums = call(
        change_kernel,
        "change",
        1.0,
        [vmem] * 3 + [hbm] * 4,
        [vmem, smem],
        [f32_blocks, jax.ShapeDtypeStruct((2,), jnp.float32)],
        [wide, dma((8,))],
    )(where, data_a, data_b, residual, *gradient)

    sums = total(sums)
    step = -sums[0] / (sums[1] + 1e-06)

    new_primaries = jnp.zeros((2, MESSAGES, rows, width), jnp.bfloat16)
    new_residual = jnp.zeros((2, MESSAGES, rows, width), jnp.float32)
    updated = [(residual[k] + step * change[k]).astype(jnp.bfloat16) for k in range(4)]
    updated = [from_home(updated[k], k) for k in range(4)]
    for k in range(4):
        old = lax.dynamic_index_in_dim(prim_blocks, z ^ k, 1, keepdims=False)
        new = old.astype(jnp.float32) + step * returned[k].astype(jnp.float32)
        new_primaries = lax.dynamic_update_index_in_dim(
            new_primaries, new.astype(jnp.bfloat16), z ^ k, 1
        )
        new_residual = lax.dynamic_update_index_in_dim(
            new_residual, updated[k].astype(jnp.float32), z ^ k, 1
        )
    return new_primaries.reshape(data.shape), new_residual.reshape(data.shape)


def solution(mesh):
    shape = tuple(mesh.shape[name] for name in ("row", "col", "freq"))
    if shape == (2, 4, 4):
        fine = Mesh(np.asarray(mesh.devices).reshape(2, 2, 2, 2, 2), FINE)
        spec = P(None, ("twin", "lane"), "row", ("half", "pair"))
        local = whole_rows
    else:
        fine, spec, local = mesh, P(None, "freq", "row", "col"), blocked
    return jax.shard_map(
        local, mesh=fine, in_specs=(spec, spec), out_specs=(spec, spec), check_vma=False
    )
```

```python
import jax
import jax.numpy as jnp
import numpy as np
from jax import lax
from jax.experimental import pallas as pl
from jax.experimental.pallas import tpu as pltpu
from jax.sharding import Mesh
from jax.sharding import PartitionSpec as P

MIB = 1024 * 1024


def batched(left, right):
    return jnp.einsum("fik,fkj->fij", left, right, preferred_element_type=jnp.float32)


def complex_product(left, right):
    real = batched(left[0], right[0]) - batched(left[1], right[1])
    imag = batched(left[0], right[1]) + batched(left[1], right[0])
    return jnp.stack([real, imag])


def blocked_gradient(data_part, primary_part):
    src_rows = data_part.shape[2]
    columns = lax.all_gather(data_part, "row", axis=2, tiled=True)

    def add_block(piece):
        return complex_product(piece, columns)

    forward = add_block(lax.all_gather(primary_part, "col", axis=3, tiled=True))
    residual = data_part.astype(jnp.float32) - primary_part.astype(jnp.float32) + forward
    rounded = residual.astype(jnp.bfloat16)
    real = jnp.einsum("fjk,fik->jfi", columns[0], rounded[0], preferred_element_type=jnp.float32)
    real = real + jnp.einsum(
        "fjk,fik->jfi", columns[1], rounded[1], preferred_element_type=jnp.float32
    )
    imag = jnp.einsum("fjk,fik->jfi", columns[0], rounded[1], preferred_element_type=jnp.float32)
    imag = imag - jnp.einsum(
        "fjk,fik->jfi", columns[1], rounded[0], preferred_element_type=jnp.float32
    )
    summed = lax.psum_scatter(
        jnp.concatenate([real, imag], axis=2), "col", scatter_dimension=0, tiled=True
    )
    adjoint = jnp.stack([summed[:, :, :src_rows], summed[:, :, src_rows:]]).transpose(0, 2, 3, 1)
    gradient = (adjoint - residual).astype(jnp.bfloat16)
    moved = add_block(lax.all_gather(gradient, "col", axis=3, tiled=True))
    change = moved - gradient.astype(jnp.float32)
    return (residual, gradient, change)


def blocked(data, primaries):
    res, grad, chg = blocked_gradient(data, primaries)
    inner_local = jnp.sum(chg * res)
    energy_local = jnp.sum(chg * chg)
    inner, energy = lax.psum((inner_local, energy_local), ("row", "col", "freq"))
    step = -inner / (energy + 1e-06)
    updated_primaries = (primaries.astype(jnp.float32) + step * grad.astype(jnp.float32)).astype(
        jnp.bfloat16
    )
    updated_residual = res + step * chg
    return (updated_primaries, updated_residual)


FINE = ("row", "half", "pair", "twin", "lane")
MESSAGES = 4
GROUPS = ((0, 1), (2, 3))
OFFSETS = tuple((dx, dp) for dx in range(2) for dp in range(4))


def send_pairs(k):
    pairs = []
    for z in range(4):
        for f in range(4):
            twin, lane, part = f // 2, f % 2, z ^ k
            pairs.append((z * 4 + f, (lane * 2 + part // 2) * 4 + twin * 2 + part % 2))
    return pairs


COLUMN = ("half", "pair", "twin", "lane")


def to_home(blocks, z, k):
    piece = lax.dynamic_index_in_dim(blocks, z ^ k, 1, keepdims=False)
    return lax.ppermute(piece, COLUMN, send_pairs(k))


def from_home(piece, k):
    return lax.ppermute(piece, COLUMN, [(b, a) for a, b in send_pairs(k)])


def swap(value, axis):
    return lax.ppermute(value, axis, [(0, 1), (1, 0)])


def total(value):
    for axis in ("lane", "row", "twin", "pair", "half"):
        value = value + swap(value, axis)
    return value


def place_copies(group, buffers, where, data_v, sems, rows):
    row_index, part = where
    copies = [[] for _ in range(4)]
    for number, ((dx, dp), buffer) in enumerate(zip(OFFSETS, buffers)):
        start = ((row_index ^ dx) * 2 + (part ^ dp) % 2) * rows
        at = pl.ds(pl.multiple_of(start, rows), rows)
        for sub, k in enumerate(group):
            target = data_v.at[dp ^ k, :, at, :]
            copies[dp ^ k].append(
                pltpu.make_async_copy(buffer.at[sub], target, sems.at[2 * number + sub])
            )
    return copies


def message_copies(refs, part, wide_v, blocks_v, sems, rows, width):
    copies = []
    for k in range(4):
        z = part ^ k
        at = pl.ds(pl.multiple_of(z // 2 * width, width), width)
        for i in range(2):
            target = wide_v.at[z % 2, pl.ds(i * rows, rows), at]
            copies.append(pltpu.make_async_copy(refs[k].at[i], target, sems.at[3 * k + i]))
        copies.append(pltpu.make_async_copy(refs[k], blocks_v.at[k], sems.at[3 * k + 2]))
    return copies


def product(stacked, right, n, rows):
    one = jnp.dot(stacked, right[n, 0], preferred_element_type=jnp.float32)
    two = jnp.dot(stacked, right[n, 1], preferred_element_type=jnp.float32)
    return one[:rows] - two[rows:], one[rows:] + two[:rows]


def against(left, right):
    dims = (((1,), (1,)), ((), ()))
    return lax.dot_general(left, right, dims, preferred_element_type=jnp.float32)


def gradient_blocks(second, part, a_v, b_v, r_v, rb_v, g_v, g_outs, sems, rows, width):
    half = part // 2
    at = pl.ds(pl.multiple_of((half ^ second) * width, width), width)
    for odd in range(2):
        one = two = None
        for t in range(4):
            source = a_v if odd == t // 2 else b_v
            first_dot = against(rb_v[t], source[t, 0, at, :])
            second_dot = against(rb_v[t], source[t, 1, at, :])
            one = first_dot if one is None else one + first_dot
            two = second_dot if two is None else two + second_dot
        slot = half ^ odd ^ part % 2
        k = slot + 2 * second
        g_v[slot, 0] = (one[:rows] + two[rows:] - r_v[k, 0]).astype(jnp.bfloat16)
        g_v[slot, 1] = (one[rows:] - two[:rows] - r_v[k, 1]).astype(jnp.bfloat16)
    outs = [pltpu.make_async_copy(g_v.at[j], g_outs[j], sems.at[j]) for j in range(2)]
    for copy in outs:
        copy.start()
    for copy in outs:
        copy.wait()


def forward_kernel(rows, width, where_ref, *refs):
    a_in, x_refs, d_refs, (f_out, wide_out) = refs[:8], refs[8:12], refs[12:16], refs[16:18]
    a_v, wide_v, x_v, d_v, f_v, sems, x_sems, d_sems, out_sems = refs[18:]
    part = where_ref[1]
    copies = place_copies(GROUPS[0], a_in, (where_ref[0], part), a_v, sems, rows)
    x_copies = message_copies(x_refs, part, wide_v, x_v, x_sems, rows, width)
    for k in range(4):
        x_copies.append(pltpu.make_async_copy(d_refs[k], d_v.at[k], d_sems.at[k]))
    for copy in copies[0] + x_copies + copies[1]:
        copy.start()
    for copy in x_copies:
        copy.wait()
    outs = [pltpu.make_async_copy(wide_v, wide_out, out_sems.at[4])]
    outs[0].start()
    for t in range(4):
        for copy in copies[t]:
            copy.wait()
        if t < 2:
            for copy in copies[t + 2]:
                copy.start()
        forward = product(wide_v[part // 2 ^ t // 2], a_v, t, rows)
        for i in range(2):
            own = d_v[t, i].astype(jnp.float32) - x_v[t, i].astype(jnp.float32)
            f_v[t, i] = own + forward[i]
        outs.append(pltpu.make_async_copy(f_v.at[t], f_out.at[t], out_sems.at[t]))
        outs[-1].start()
    for copy in outs:
        copy.wait()


def residual_kernel(rows, width, where_ref, *refs):
    a_in, b_in, (wide_in, f_in), refs = refs[:8], refs[8:16], refs[16:18], refs[18:]
    a_v, b_v, r_v, rb_v, g0, g1, wide_v, f_v, g_v, a_sems, b_sems, in_sems, out_sems = refs
    where = (where_ref[0], where_ref[1])
    part = where[1]
    copies = place_copies(GROUPS[1], b_in, where, b_v, b_sems, rows)
    later = place_copies(GROUPS[0], a_in, where, a_v, a_sems, rows)
    for t in range(4):
        copies[t].append(pltpu.make_async_copy(f_in.at[t], f_v.at[t], in_sems.at[t]))
    copies[0].append(pltpu.make_async_copy(wide_in, wide_v, in_sems.at[4]))
    for copy in copies[0] + copies[1]:
        copy.start()
    for t in range(4):
        for copy in copies[t]:
            copy.wait()
        for copy in copies[t + 2] if t < 2 else later[2 * t - 4] + later[2 * t - 3]:
            copy.start()
        forward = product(wide_v[1 - (part // 2 ^ t // 2)], b_v, t, rows)
        for i in range(2):
            residual = f_v[t, i] + forward[i]
            r_v[t, i] = residual
            rb_v[t, i * rows : (i + 1) * rows, :] = residual.astype(jnp.bfloat16)
    for t in range(4):
        for copy in later[t]:
            copy.wait()
    gradient_blocks(0, part, a_v, b_v, r_v, rb_v, g_v, (g0, g1), out_sems, rows, width)


def gradient_kernel(rows, width, where_ref, a_v, b_v, r_v, rb_v, g2, g3, g_v, out_sems):
    part = where_ref[1]
    gradient_blocks(1, part, a_v, b_v, r_v, rb_v, g_v, (g2, g3), out_sems, rows, width)


def change_kernel(rows, width, where_ref, a_v, b_v, r_v, *refs):
    g_refs, (c_v, sums_out, wide_v, g_v, g_sems) = refs[:4], refs[4:]
    part = where_ref[1]
    g_copies = message_copies(g_refs, part, wide_v, g_v, g_sems, rows, width)
    for copy in g_copies:
        copy.start()
    for copy in g_copies:
        copy.wait()
    inner = jnp.zeros((rows, width), jnp.float32)
    energy = jnp.zeros((rows, width), jnp.float32)
    for t in range(4):
        pair = part // 2 ^ t // 2
        from_a = product(wide_v[pair], a_v, t, rows)
        from_b = product(wide_v[1 - pair], b_v, t, rows)
        for i in range(2):
            change = from_a[i] + from_b[i] - g_v[t, i].astype(jnp.float32)
            c_v[t, i] = change
            inner = inner + change * r_v[t, i]
            energy = energy + change * change
    sums_out[0] = jnp.sum(inner)
    sums_out[1] = jnp.sum(energy)


def whole_rows(data, primaries):
    z = lax.axis_index("half") * 2 + lax.axis_index("pair")
    part = lax.axis_index("pair") * 2 + lax.axis_index("lane")
    n_rows, width = data.shape[2], data.shape[3]
    rows = n_rows // MESSAGES
    where = jnp.stack([lax.axis_index("row"), part]).astype(jnp.int32)
    data_blocks = data.reshape(2, MESSAGES, rows, width)
    prim_blocks = primaries.reshape(2, MESSAGES, rows, width)

    arrived = [to_home(data_blocks, z, k) for k in range(MESSAGES)]
    buffers, by_pair = [], []
    for group in GROUPS:
        own = jnp.stack([arrived[k] for k in group])
        held = {(0, 0): own, (0, 2): swap(own, "pair")}
        by_pair.append(held[0, 2])
        held.update({(1, dp): swap(v, "row") for (_, dp), v in list(held.items())})
        held.update({(dx, dp ^ 1): swap(v, "lane") for (dx, dp), v in list(held.items())})
        buffers.append(
            [pltpu.with_memory_space_constraint(held[at], pltpu.HBM) for at in OFFSETS]
        )
    x_parts = []
    for k, ready in enumerate((arrived, by_pair[0], by_pair[1], by_pair[1])):
        later, _ = lax.optimization_barrier((prim_blocks, ready))
        x_parts.append(to_home(later, z, k))

    hbm = pl.BlockSpec(memory_space=pltpu.HBM)
    vmem = pl.BlockSpec(memory_space=pltpu.VMEM)
    smem = pl.BlockSpec(memory_space=pltpu.SMEM)
    message = jax.ShapeDtypeStruct((2, rows, width), jnp.bfloat16)
    f32_blocks = pltpu.VMEM((4, 2, rows, width), jnp.float32)
    data_half = pltpu.VMEM((4, 2, 4 * rows, width), jnp.bfloat16)
    wide = pltpu.VMEM((2, 2 * rows, 2 * width), jnp.bfloat16)
    blocks = pltpu.VMEM((4, 2, rows, width), jnp.bfloat16)
    rounded = pltpu.VMEM((4, 2 * rows, width), jnp.bfloat16)
    two_messages = pltpu.VMEM((2, 2, rows, width), jnp.bfloat16)
    dma = pltpu.SemaphoreType.DMA
    one_product = 8 * rows * (4 * width) * (4 * width)

    def call(kernel, name, products, mib, in_specs, out_specs, out_shape, scratch):
        return pl.pallas_call(
            lambda *refs: kernel(rows, width, *refs),
            in_specs=[smem] + in_specs,
            out_specs=out_specs,
            out_shape=out_shape,
            scratch_shapes=scratch,
            compiler_params=pltpu.CompilerParams(vmem_limit_bytes=mib * MIB),
            cost_estimate=pl.CostEstimate(
                flops=int(products * one_product), transcendentals=0, bytes_accessed=1 << 24
            ),
            name=name,
        )

    partial, x_wide = call(
        forward_kernel,
        "forward",
        0.5,
        26,
        [hbm] * 16,
        [hbm] * 2,
        [
            pltpu.HBM((4, 2, rows, width), jnp.float32),
            pltpu.HBM((2, 2 * rows, 2 * width), jnp.bfloat16),
        ],
        [
            data_half,
            wide,
            blocks,
            blocks,
            f32_blocks,
            dma((16,)),
            dma((12,)),
            dma((4,)),
            dma((5,)),
        ],
    )(where, *buffers[0], *x_parts, *arrived)
    data_a, data_b, residual, res_rounded, g0, g1 = call(
        residual_kernel,
        "residual",
        1.0,
        14,
        [hbm] * 18,
        [vmem] * 4 + [hbm] * 2,
        [data_half, data_half, f32_blocks, rounded, message, message],
        [wide, f32_blocks, two_messages, dma((16,)), dma((16,)), dma((5,)), dma((2,))],
    )(where, *buffers[0], *buffers[1], x_wide, partial)
    g2, g3 = call(
        gradient_kernel,
        "gradient",
        0.5,
        8,
        [vmem] * 4,
        [hbm] * 2,
        [message, message],
        [two_messages, dma((2,))],
    )(where, data_a, data_b, residual, res_rounded)
    gradient = [g0, g1, g2, g3]
    returned = [from_home(gradient[k], k) for k in range(4)]
    change, sums = call(
        change_kernel,
        "change",
        1.0,
        12,
        [vmem] * 3 + [hbm] * 4,
        [vmem, smem],
        [f32_blocks, jax.ShapeDtypeStruct((2,), jnp.float32)],
        [wide, blocks, dma((12,))],
    )(where, data_a, data_b, residual, *gradient)

    sums = total(sums)
    step = -sums[0] / (sums[1] + 1e-06)

    new_primaries = jnp.zeros((2, MESSAGES, rows, width), jnp.bfloat16)
    new_residual = jnp.zeros((2, MESSAGES, rows, width), jnp.float32)
    updated = [(residual[k] + step * change[k]).astype(jnp.bfloat16) for k in range(4)]
    updated = [from_home(updated[k], k) for k in range(4)]
    for k in range(4):
        old = lax.dynamic_index_in_dim(prim_blocks, z ^ k, 1, keepdims=False)
        new = old.astype(jnp.float32) + step * returned[k].astype(jnp.float32)
        new_primaries = lax.dynamic_update_index_in_dim(
            new_primaries, new.astype(jnp.bfloat16), z ^ k, 1
        )
        new_residual = lax.dynamic_update_index_in_dim(
            new_residual, updated[k].astype(jnp.float32), z ^ k, 1
        )
    return new_primaries.reshape(data.shape), new_residual.reshape(data.shape)


def solution(mesh):
    shape = tuple(mesh.shape[name] for name in ("row", "col", "freq"))
    if shape == (2, 4, 4):
        fine = Mesh(np.asarray(mesh.devices).reshape(2, 2, 2, 2, 2), FINE)
        spec = P(None, ("twin", "lane"), "row", ("half", "pair"))
        local = whole_rows
    else:
        fine, spec, local = mesh, P(None, "freq", "row", "col"), blocked
    return jax.shard_map(
        local, mesh=fine, in_specs=(spec, spec), out_specs=(spec, spec), check_vma=False
    )
```

```python
import jax
import jax.numpy as jnp
import numpy as np
from jax import lax
from jax.experimental import pallas as pl
from jax.experimental.pallas import tpu as pltpu
from jax.sharding import Mesh
from jax.sharding import PartitionSpec as P

MIB = 1024 * 1024


def batched(left, right):
    return jnp.einsum("fik,fkj->fij", left, right, preferred_element_type=jnp.float32)


def complex_product(left, right):
    real = batched(left[0], right[0]) - batched(left[1], right[1])
    imag = batched(left[0], right[1]) + batched(left[1], right[0])
    return jnp.stack([real, imag])


def blocked_gradient(data_part, primary_part):
    src_rows = data_part.shape[2]
    columns = lax.all_gather(data_part, "row", axis=2, tiled=True)

    def add_block(piece):
        return complex_product(piece, columns)

    forward = add_block(lax.all_gather(primary_part, "col", axis=3, tiled=True))
    residual = data_part.astype(jnp.float32) - primary_part.astype(jnp.float32) + forward
    rounded = residual.astype(jnp.bfloat16)
    real = jnp.einsum("fjk,fik->jfi", columns[0], rounded[0], preferred_element_type=jnp.float32)
    real = real + jnp.einsum(
        "fjk,fik->jfi", columns[1], rounded[1], preferred_element_type=jnp.float32
    )
    imag = jnp.einsum("fjk,fik->jfi", columns[0], rounded[1], preferred_element_type=jnp.float32)
    imag = imag - jnp.einsum(
        "fjk,fik->jfi", columns[1], rounded[0], preferred_element_type=jnp.float32
    )
    summed = lax.psum_scatter(
        jnp.concatenate([real, imag], axis=2), "col", scatter_dimension=0, tiled=True
    )
    adjoint = jnp.stack([summed[:, :, :src_rows], summed[:, :, src_rows:]]).transpose(0, 2, 3, 1)
    gradient = (adjoint - residual).astype(jnp.bfloat16)
    moved = add_block(lax.all_gather(gradient, "col", axis=3, tiled=True))
    change = moved - gradient.astype(jnp.float32)
    return (residual, gradient, change)


def blocked(data, primaries):
    res, grad, chg = blocked_gradient(data, primaries)
    inner_local = jnp.sum(chg * res)
    energy_local = jnp.sum(chg * chg)
    inner, energy = lax.psum((inner_local, energy_local), ("row", "col", "freq"))
    step = -inner / (energy + 1e-06)
    updated_primaries = (primaries.astype(jnp.float32) + step * grad.astype(jnp.float32)).astype(
        jnp.bfloat16
    )
    updated_residual = res + step * chg
    return (updated_primaries, updated_residual)


FINE = ("row", "half", "pair", "twin", "lane")
MESSAGES = 4
GROUPS = ((0, 1), (2, 3))
OFFSETS = tuple((dx, dp) for dx in range(2) for dp in range(4))


def send_pairs(k):
    pairs = []
    for z in range(4):
        for f in range(4):
            twin, lane, part = f // 2, f % 2, z ^ k
            pairs.append((z * 4 + f, (lane * 2 + part // 2) * 4 + twin * 2 + part % 2))
    return pairs


COLUMN = ("half", "pair", "twin", "lane")


def to_home(blocks, z, k):
    piece = lax.dynamic_index_in_dim(blocks, z ^ k, 1, keepdims=False)
    return lax.ppermute(piece, COLUMN, send_pairs(k))


def from_home(piece, k):
    return lax.ppermute(piece, COLUMN, [(b, a) for a, b in send_pairs(k)])


def swap(value, axis):
    return lax.ppermute(value, axis, [(0, 1), (1, 0)])


def pinned(value):
    return pltpu.with_memory_space_constraint(value, pltpu.HBM)


def total(value):
    for axis in ("lane", "row", "twin", "pair", "half"):
        value = value + swap(value, axis)
    return value


def place_copies(group, buffers, where, data_v, sems, rows):
    row_index, part = where
    copies = [[] for _ in range(4)]
    for number, ((dx, dp), buffer) in enumerate(zip(OFFSETS, buffers)):
        start = ((row_index ^ dx) * 2 + (part ^ dp) % 2) * rows
        at = pl.ds(pl.multiple_of(start, rows), rows)
        for sub, k in enumerate(group):
            target = data_v.at[dp ^ k, :, at, :]
            copies[dp ^ k].append(
                pltpu.make_async_copy(buffer.at[sub], target, sems.at[2 * number + sub])
            )
    return copies


def message_copies(refs, part, wide_v, blocks_v, sems, rows, width):
    copies = []
    for k in range(4):
        z = part ^ k
        at = pl.ds(pl.multiple_of(z // 2 * width, width), width)
        for i in range(2):
            target = wide_v.at[z % 2, pl.ds(i * rows, rows), at]
            copies.append(pltpu.make_async_copy(refs[k].at[i], target, sems.at[3 * k + i]))
        copies.append(pltpu.make_async_copy(refs[k], blocks_v.at[k], sems.at[3 * k + 2]))
    return copies


def product(stacked, right, n, rows):
    one = jnp.dot(stacked, right[n, 0], preferred_element_type=jnp.float32)
    two = jnp.dot(stacked, right[n, 1], preferred_element_type=jnp.float32)
    return one[:rows] - two[rows:], one[rows:] + two[:rows]


def against(left, right):
    dims = (((1,), (1,)), ((), ()))
    return lax.dot_general(left, right, dims, preferred_element_type=jnp.float32)


def gradient_blocks(second, part, a_v, b_v, r_v, rb_v, g_v, g_outs, sems, rows, width):
    half = part // 2
    at = pl.ds(pl.multiple_of((half ^ second) * width, width), width)
    for odd in range(2):
        one = two = None
        for t in range(4):
            source = a_v if odd == t // 2 else b_v
            first_dot = against(rb_v[t], source[t, 0, at, :])
            second_dot = against(rb_v[t], source[t, 1, at, :])
            one = first_dot if one is None else one + first_dot
            two = second_dot if two is None else two + second_dot
        slot = half ^ odd ^ part % 2
        k = slot + 2 * second
        g_v[slot, 0] = (one[:rows] + two[rows:] - r_v[k, 0]).astype(jnp.bfloat16)
        g_v[slot, 1] = (one[rows:] - two[:rows] - r_v[k, 1]).astype(jnp.bfloat16)
    outs = [pltpu.make_async_copy(g_v.at[j], g_outs[j], sems.at[j]) for j in range(2)]
    for copy in outs:
        copy.start()
    for copy in outs:
        copy.wait()


def collect_kernel(rows, width, where_ref, *refs):
    a_in, (a_v, sems) = refs[:8], refs[8:]
    copies = place_copies(GROUPS[0], a_in, (where_ref[0], where_ref[1]), a_v, sems, rows)
    for t in range(4):
        for copy in copies[t]:
            copy.start()
    for t in range(4):
        for copy in copies[t]:
            copy.wait()


def residual_kernel(rows, width, where_ref, a_v, *refs):
    b_in, x_refs, d_refs, refs = refs[:8], refs[8:12], refs[12:16], refs[16:]
    b_v, r_v, rb_v, g0, g1, wide_v, x_v, d_v, g_v, b_sems, x_sems, d_sems, out_sems = refs
    where = (where_ref[0], where_ref[1])
    part = where[1]
    copies = place_copies(GROUPS[1], b_in, where, b_v, b_sems, rows)
    x_copies = message_copies(x_refs, part, wide_v, x_v, x_sems, rows, width)
    for k in range(4):
        copies[0].append(pltpu.make_async_copy(d_refs[k], d_v.at[k], d_sems.at[k]))
    copies[0] += [x_copies[3 * k + 2] for k in range(4)]
    wide_copies = [x_copies[3 * k + i] for k in range(4) for i in range(2)]
    for copy in wide_copies:
        copy.start()
    for copy in wide_copies:
        copy.wait()
    for t in range(4):
        for copy in copies[t]:
            copy.start()
    for t in range(4):
        forward = product(wide_v[part // 2 ^ t // 2], a_v, t, rows)
        for i in range(2):
            r_v[t, i] = forward[i]
    for t in range(4):
        for copy in copies[t]:
            copy.wait()
        forward = product(wide_v[1 - (part // 2 ^ t // 2)], b_v, t, rows)
        for i in range(2):
            own = d_v[t, i].astype(jnp.float32) - x_v[t, i].astype(jnp.float32)
            residual = own + (r_v[t, i] + forward[i])
            r_v[t, i] = residual
            rb_v[t, i * rows : (i + 1) * rows, :] = residual.astype(jnp.bfloat16)
    gradient_blocks(0, part, a_v, b_v, r_v, rb_v, g_v, (g0, g1), out_sems, rows, width)


def gradient_kernel(rows, width, where_ref, a_v, b_v, r_v, rb_v, g2, g3, g_v, out_sems):
    part = where_ref[1]
    gradient_blocks(1, part, a_v, b_v, r_v, rb_v, g_v, (g2, g3), out_sems, rows, width)


def change_kernel(rows, width, where_ref, a_v, b_v, r_v, *refs):
    g_refs, (c_v, sums_out, wide_v, g_v, g_sems) = refs[:4], refs[4:]
    part = where_ref[1]
    g_copies = message_copies(g_refs, part, wide_v, g_v, g_sems, rows, width)
    for copy in g_copies:
        copy.start()
    for copy in g_copies:
        copy.wait()
    inner = jnp.zeros((rows, width), jnp.float32)
    energy = jnp.zeros((rows, width), jnp.float32)
    for t in range(4):
        pair = part // 2 ^ t // 2
        from_a = product(wide_v[pair], a_v, t, rows)
        from_b = product(wide_v[1 - pair], b_v, t, rows)
        for i in range(2):
            change = from_a[i] + from_b[i] - g_v[t, i].astype(jnp.float32)
            c_v[t, i] = change
            inner = inner + change * r_v[t, i]
            energy = energy + change * change
    sums_out[0] = jnp.sum(inner)
    sums_out[1] = jnp.sum(energy)


def whole_rows(data, primaries):
    z = lax.axis_index("half") * 2 + lax.axis_index("pair")
    part = lax.axis_index("pair") * 2 + lax.axis_index("lane")
    n_rows, width = data.shape[2], data.shape[3]
    rows = n_rows // MESSAGES
    where = jnp.stack([lax.axis_index("row"), part]).astype(jnp.int32)
    data_blocks = data.reshape(2, MESSAGES, rows, width)
    prim_blocks = primaries.reshape(2, MESSAGES, rows, width)

    arrived = [to_home(data_blocks, z, k) for k in range(MESSAGES)]
    held = []
    for group in GROUPS:
        own = jnp.stack([arrived[k] for k in group])
        pieces = {(0, 0): own, (0, 2): swap(own, "pair"), (1, 0): swap(own, "row")}
        pieces[1, 2] = swap(pieces[0, 2], "row")
        held.append(pieces)
    ready = [[arrived, held[0][1, 0]], [held[1][1, 0], held[0][0, 2]], [held[1][0, 2]], [held[1][0, 2]]]
    x_parts = []
    for k in range(MESSAGES):
        later, _ = lax.optimization_barrier((prim_blocks, ready[k]))
        x_parts.append(to_home(later, z, k))

    def complete(pieces, after):
        for at, value in list(pieces.items()):
            if at != (1, 2):
                value, _ = lax.optimization_barrier((value, after))
            pieces[at[0], at[1] ^ 1] = swap(value, "lane")
        return [pinned(pieces[at]) for at in OFFSETS]

    held[1][1, 2], _ = lax.optimization_barrier((held[1][1, 2], x_parts))
    first_buffers = complete(held[0], held[0][1, 2])
    second_buffers = complete(held[1], first_buffers[3])

    hbm = pl.BlockSpec(memory_space=pltpu.HBM)
    vmem = pl.BlockSpec(memory_space=pltpu.VMEM)
    smem = pl.BlockSpec(memory_space=pltpu.SMEM)
    message = jax.ShapeDtypeStruct((2, rows, width), jnp.bfloat16)
    f32_blocks = pltpu.VMEM((4, 2, rows, width), jnp.float32)
    data_half = pltpu.VMEM((4, 2, 4 * rows, width), jnp.bfloat16)
    wide = pltpu.VMEM((2, 2 * rows, 2 * width), jnp.bfloat16)
    blocks = pltpu.VMEM((4, 2, rows, width), jnp.bfloat16)
    rounded = pltpu.VMEM((4, 2 * rows, width), jnp.bfloat16)
    two_messages = pltpu.VMEM((2, 2, rows, width), jnp.bfloat16)
    dma = pltpu.SemaphoreType.DMA
    one_product = 8 * rows * (4 * width) * (4 * width)

    def call(kernel, name, products, mib, in_specs, out_specs, out_shape, scratch):
        return pl.pallas_call(
            lambda *refs: kernel(rows, width, *refs),
            in_specs=[smem] + in_specs,
            out_specs=out_specs,
            out_shape=out_shape,
            scratch_shapes=scratch,
            compiler_params=pltpu.CompilerParams(vmem_limit_bytes=mib * MIB),
            cost_estimate=pl.CostEstimate(
                flops=int(products * one_product), transcendentals=0, bytes_accessed=1 << 24
            ),
            name=name,
        )

    data_a = call(
        collect_kernel, "collect", 0.1, 2, [hbm] * 8, vmem, data_half, [dma((16,))]
    )(where, *first_buffers)
    data_b, residual, res_rounded, g0, g1 = call(
        residual_kernel,
        "residual",
        1.5,
        16,
        [vmem] + [hbm] * 16,
        [vmem] * 3 + [hbm] * 2,
        [data_half, f32_blocks, rounded, message, message],
        [
            wide,
            blocks,
            blocks,
            two_messages,
            dma((16,)),
            dma((12,)),
            dma((4,)),
            dma((2,)),
        ],
    )(where, data_a, *second_buffers, *map(pinned, x_parts), *map(pinned, arrived))
    g2, g3 = call(
        gradient_kernel,
        "gradient",
        0.5,
        8,
        [vmem] * 4,
        [hbm] * 2,
        [message, message],
        [two_messages, dma((2,))],
    )(where, data_a, data_b, residual, res_rounded)
    gradient = [g0, g1, g2, g3]
    returned = [from_home(gradient[k], k) for k in range(4)]
    change, sums = call(
        change_kernel,
        "change",
        1.0,
        12,
        [vmem] * 3 + [hbm] * 4,
        [vmem, smem],
        [f32_blocks, jax.ShapeDtypeStruct((2,), jnp.float32)],
        [wide, blocks, dma((12,))],
    )(where, data_a, data_b, residual, *gradient)

    sums = total(sums)
    step = -sums[0] / (sums[1] + 1e-06)

    new_primaries = jnp.zeros((2, MESSAGES, rows, width), jnp.bfloat16)
    new_residual = jnp.zeros((2, MESSAGES, rows, width), jnp.float32)
    updated = [(residual[k] + step * change[k]).astype(jnp.bfloat16) for k in range(4)]
    updated = [from_home(updated[k], k) for k in range(4)]
    for k in range(4):
        old = lax.dynamic_index_in_dim(prim_blocks, z ^ k, 1, keepdims=False)
        new = old.astype(jnp.float32) + step * returned[k].astype(jnp.float32)
        new_primaries = lax.dynamic_update_index_in_dim(
            new_primaries, new.astype(jnp.bfloat16), z ^ k, 1
        )
        new_residual = lax.dynamic_update_index_in_dim(
            new_residual, updated[k].astype(jnp.float32), z ^ k, 1
        )
    return new_primaries.reshape(data.shape), new_residual.reshape(data.shape)


def solution(mesh):
    shape = tuple(mesh.shape[name] for name in ("row", "col", "freq"))
    if shape == (2, 4, 4):
        fine = Mesh(np.asarray(mesh.devices).reshape(2, 2, 2, 2, 2), FINE)
        spec = P(None, ("twin", "lane"), "row", ("half", "pair"))
        local = whole_rows
    else:
        fine, spec, local = mesh, P(None, "freq", "row", "col"), blocked
    return jax.shard_map(
        local, mesh=fine, in_specs=(spec, spec), out_specs=(spec, spec), check_vma=False
    )
```

```python
import jax
import jax.numpy as jnp
import numpy as np
from jax import lax
from jax.experimental import pallas as pl
from jax.experimental.pallas import tpu as pltpu
from jax.sharding import Mesh
from jax.sharding import PartitionSpec as P

MIB = 1024 * 1024


def batched(left, right):
    return jnp.einsum("fik,fkj->fij", left, right, preferred_element_type=jnp.float32)


def complex_product(left, right):
    real = batched(left[0], right[0]) - batched(left[1], right[1])
    imag = batched(left[0], right[1]) + batched(left[1], right[0])
    return jnp.stack([real, imag])


def blocked_gradient(data_part, primary_part):
    src_rows = data_part.shape[2]
    columns = lax.all_gather(data_part, "row", axis=2, tiled=True)

    def add_block(piece):
        return complex_product(piece, columns)

    forward = add_block(lax.all_gather(primary_part, "col", axis=3, tiled=True))
    residual = data_part.astype(jnp.float32) - primary_part.astype(jnp.float32) + forward
    rounded = residual.astype(jnp.bfloat16)
    real = jnp.einsum("fjk,fik->jfi", columns[0], rounded[0], preferred_element_type=jnp.float32)
    real = real + jnp.einsum(
        "fjk,fik->jfi", columns[1], rounded[1], preferred_element_type=jnp.float32
    )
    imag = jnp.einsum("fjk,fik->jfi", columns[0], rounded[1], preferred_element_type=jnp.float32)
    imag = imag - jnp.einsum(
        "fjk,fik->jfi", columns[1], rounded[0], preferred_element_type=jnp.float32
    )
    summed = lax.psum_scatter(
        jnp.concatenate([real, imag], axis=2), "col", scatter_dimension=0, tiled=True
    )
    adjoint = jnp.stack([summed[:, :, :src_rows], summed[:, :, src_rows:]]).transpose(0, 2, 3, 1)
    gradient = (adjoint - residual).astype(jnp.bfloat16)
    moved = add_block(lax.all_gather(gradient, "col", axis=3, tiled=True))
    change = moved - gradient.astype(jnp.float32)
    return (residual, gradient, change)


def blocked(data, primaries):
    res, grad, chg = blocked_gradient(data, primaries)
    inner_local = jnp.sum(chg * res)
    energy_local = jnp.sum(chg * chg)
    inner, energy = lax.psum((inner_local, energy_local), ("row", "col", "freq"))
    step = -inner / (energy + 1e-06)
    updated_primaries = (primaries.astype(jnp.float32) + step * grad.astype(jnp.float32)).astype(
        jnp.bfloat16
    )
    updated_residual = res + step * chg
    return (updated_primaries, updated_residual)


FINE = ("row", "half", "pair", "twin", "lane")
MESSAGES = 4
GROUPS = ((0, 1), (2, 3))
OFFSETS = tuple((dx, dp) for dx in range(2) for dp in range(4))


def send_pairs(k):
    pairs = []
    for z in range(4):
        for f in range(4):
            twin, lane, part = f // 2, f % 2, z ^ k
            pairs.append((z * 4 + f, (lane * 2 + part // 2) * 4 + twin * 2 + part % 2))
    return pairs


COLUMN = ("half", "pair", "twin", "lane")


def to_home(blocks, z, k):
    piece = lax.dynamic_index_in_dim(blocks, z ^ k, 1, keepdims=False)
    return lax.ppermute(piece, COLUMN, send_pairs(k))


def from_home(piece, k):
    return lax.ppermute(piece, COLUMN, [(b, a) for a, b in send_pairs(k)])


def swap(value, axis):
    return lax.ppermute(value, axis, [(0, 1), (1, 0)])


def pinned(value):
    return pltpu.with_memory_space_constraint(value, pltpu.HBM)


def total(value):
    for axis in ("lane", "row", "twin", "pair", "half"):
        value = value + swap(value, axis)
    return value


def place_copies(group, buffers, where, data_v, sems, rows):
    row_index, part = where
    copies = [[] for _ in range(4)]
    for number, ((dx, dp), buffer) in enumerate(zip(OFFSETS, buffers)):
        start = ((row_index ^ dx) * 2 + (part ^ dp) % 2) * rows
        at = pl.ds(pl.multiple_of(start, rows), rows)
        for sub, k in enumerate(group):
            target = data_v.at[dp ^ k, :, at, :]
            copies[dp ^ k].append(
                pltpu.make_async_copy(buffer.at[sub], target, sems.at[2 * number + sub])
            )
    return copies


def message_copies(refs, part, wide_v, blocks_v, sems, rows, width):
    copies = []
    for k in range(4):
        z = part ^ k
        at = pl.ds(pl.multiple_of(z // 2 * width, width), width)
        for i in range(2):
            target = wide_v.at[z % 2, pl.ds(i * rows, rows), at]
            copies.append(pltpu.make_async_copy(refs[k].at[i], target, sems.at[3 * k + i]))
        copies.append(pltpu.make_async_copy(refs[k], blocks_v.at[k], sems.at[3 * k + 2]))
    return copies


def product(stacked, right, n, rows):
    one = jnp.dot(stacked, right[n, 0], preferred_element_type=jnp.float32)
    two = jnp.dot(stacked, right[n, 1], preferred_element_type=jnp.float32)
    return one[:rows] - two[rows:], one[rows:] + two[:rows]


def against(left, right):
    dims = (((1,), (1,)), ((), ()))
    return lax.dot_general(left, right, dims, preferred_element_type=jnp.float32)


def gradient_blocks(second, part, a_v, b_v, r_v, rb_v, g_v, g_outs, sems, rows, width):
    half = part // 2
    at = pl.ds(pl.multiple_of((half ^ second) * width, width), width)
    for odd in range(2):
        one = two = None
        for t in range(4):
            source = a_v if odd == t // 2 else b_v
            first_dot = against(rb_v[t], source[t, 0, at, :])
            second_dot = against(rb_v[t], source[t, 1, at, :])
            one = first_dot if one is None else one + first_dot
            two = second_dot if two is None else two + second_dot
        slot = half ^ odd ^ part % 2
        k = slot + 2 * second
        g_v[slot, 0] = (one[:rows] + two[rows:] - r_v[k, 0]).astype(jnp.bfloat16)
        g_v[slot, 1] = (one[rows:] - two[:rows] - r_v[k, 1]).astype(jnp.bfloat16)
    outs = [pltpu.make_async_copy(g_v.at[j], g_outs[j], sems.at[j]) for j in range(2)]
    for copy in outs:
        copy.start()
    for copy in outs:
        copy.wait()


def collect_kernel(rows, width, where_ref, *refs):
    a_in, x_refs, d_refs, refs = refs[:8], refs[8:12], refs[12:16], refs[16:]
    a_v, wide_v, f_v, x_v, d_v, sems, x_sems, d_sems = refs
    part = where_ref[1]
    copies = place_copies(GROUPS[0], a_in, (where_ref[0], part), a_v, sems, rows)
    x_copies = message_copies(x_refs, part, wide_v, x_v, x_sems, rows, width)
    for k in range(4):
        x_copies.append(pltpu.make_async_copy(d_refs[k], d_v.at[k], d_sems.at[k]))
    for copy in copies[0] + x_copies + copies[1]:
        copy.start()
    for copy in x_copies:
        copy.wait()
    for t in range(4):
        for copy in copies[t]:
            copy.wait()
        if t < 2:
            for copy in copies[t + 2]:
                copy.start()
        forward = product(wide_v[part // 2 ^ t // 2], a_v, t, rows)
        for i in range(2):
            own = d_v[t, i].astype(jnp.float32) - x_v[t, i].astype(jnp.float32)
            f_v[t, i] = own + forward[i]


def residual_kernel(rows, width, where_ref, a_v, wide_v, f_v, *refs):
    b_in, (b_v, r_v, rb_v, g0, g1, g_v, b_sems, out_sems) = refs[:8], refs[8:]
    where = (where_ref[0], where_ref[1])
    part = where[1]
    copies = place_copies(GROUPS[1], b_in, where, b_v, b_sems, rows)
    for copy in copies[0] + copies[1]:
        copy.start()
    for t in range(4):
        for copy in copies[t]:
            copy.wait()
        if t < 2:
            for copy in copies[t + 2]:
                copy.start()
        forward = product(wide_v[1 - (part // 2 ^ t // 2)], b_v, t, rows)
        for i in range(2):
            residual = f_v[t, i] + forward[i]
            r_v[t, i] = residual
            rb_v[t, i * rows : (i + 1) * rows, :] = residual.astype(jnp.bfloat16)
    gradient_blocks(0, part, a_v, b_v, r_v, rb_v, g_v, (g0, g1), out_sems, rows, width)


def gradient_kernel(rows, width, where_ref, a_v, b_v, r_v, rb_v, g2, g3, g_v, out_sems):
    part = where_ref[1]
    gradient_blocks(1, part, a_v, b_v, r_v, rb_v, g_v, (g2, g3), out_sems, rows, width)


def change_kernel(rows, width, where_ref, a_v, b_v, r_v, *refs):
    g_refs, (c_v, sums_out, wide_v, g_v, g_sems) = refs[:4], refs[4:]
    part = where_ref[1]
    g_copies = message_copies(g_refs, part, wide_v, g_v, g_sems, rows, width)
    for copy in g_copies:
        copy.start()
    for copy in g_copies:
        copy.wait()
    inner = jnp.zeros((rows, width), jnp.float32)
    energy = jnp.zeros((rows, width), jnp.float32)
    for t in range(4):
        pair = part // 2 ^ t // 2
        from_a = product(wide_v[pair], a_v, t, rows)
        from_b = product(wide_v[1 - pair], b_v, t, rows)
        for i in range(2):
            change = from_a[i] + from_b[i] - g_v[t, i].astype(jnp.float32)
            c_v[t, i] = change
            inner = inner + change * r_v[t, i]
            energy = energy + change * change
    sums_out[0] = jnp.sum(inner)
    sums_out[1] = jnp.sum(energy)


def whole_rows(data, primaries):
    z = lax.axis_index("half") * 2 + lax.axis_index("pair")
    part = lax.axis_index("pair") * 2 + lax.axis_index("lane")
    n_rows, width = data.shape[2], data.shape[3]
    rows = n_rows // MESSAGES
    where = jnp.stack([lax.axis_index("row"), part]).astype(jnp.int32)
    data_blocks = data.reshape(2, MESSAGES, rows, width)
    prim_blocks = primaries.reshape(2, MESSAGES, rows, width)

    arrived = [to_home(data_blocks, z, k) for k in range(MESSAGES)]
    held = []
    for group in GROUPS:
        own = jnp.stack([arrived[k] for k in group])
        pieces = {(0, 0): own, (0, 2): swap(own, "pair"), (1, 0): swap(own, "row")}
        pieces[1, 2] = swap(pieces[0, 2], "row")
        held.append(pieces)
    ready = [[arrived, held[0][1, 0]], [held[1][1, 0], held[0][0, 2]], [held[1][0, 2]], [held[1][0, 2]]]
    x_parts = []
    for k in range(MESSAGES):
        later, _ = lax.optimization_barrier((prim_blocks, ready[k]))
        x_parts.append(to_home(later, z, k))

    def complete(pieces, after):
        for at, value in list(pieces.items()):
            if at != (1, 2):
                value, _ = lax.optimization_barrier((value, after))
            pieces[at[0], at[1] ^ 1] = swap(value, "lane")
        return [pinned(pieces[at]) for at in OFFSETS]

    held[1][1, 2], _ = lax.optimization_barrier((held[1][1, 2], x_parts))
    first_buffers = complete(held[0], [held[0][1, 2], x_parts[1]])
    second_buffers = complete(held[1], first_buffers[3])

    hbm = pl.BlockSpec(memory_space=pltpu.HBM)
    vmem = pl.BlockSpec(memory_space=pltpu.VMEM)
    smem = pl.BlockSpec(memory_space=pltpu.SMEM)
    message = jax.ShapeDtypeStruct((2, rows, width), jnp.bfloat16)
    f32_blocks = pltpu.VMEM((4, 2, rows, width), jnp.float32)
    data_half = pltpu.VMEM((4, 2, 4 * rows, width), jnp.bfloat16)
    wide = pltpu.VMEM((2, 2 * rows, 2 * width), jnp.bfloat16)
    blocks = pltpu.VMEM((4, 2, rows, width), jnp.bfloat16)
    rounded = pltpu.VMEM((4, 2 * rows, width), jnp.bfloat16)
    two_messages = pltpu.VMEM((2, 2, rows, width), jnp.bfloat16)
    dma = pltpu.SemaphoreType.DMA
    one_product = 8 * rows * (4 * width) * (4 * width)

    def call(kernel, name, products, mib, in_specs, out_specs, out_shape, scratch):
        return pl.pallas_call(
            lambda *refs: kernel(rows, width, *refs),
            in_specs=[smem] + in_specs,
            out_specs=out_specs,
            out_shape=out_shape,
            scratch_shapes=scratch,
            compiler_params=pltpu.CompilerParams(vmem_limit_bytes=mib * MIB),
            cost_estimate=pl.CostEstimate(
                flops=int(products * one_product), transcendentals=0, bytes_accessed=1 << 24
            ),
            name=name,
        )

    data_a, x_wide, partial = call(
        collect_kernel,
        "collect",
        0.5,
        13,
        [hbm] * 16,
        [vmem] * 3,
        [data_half, wide, f32_blocks],
        [blocks, blocks, dma((16,)), dma((12,)), dma((4,))],
    )(where, *first_buffers, *map(pinned, x_parts), *map(pinned, arrived))
    data_b, residual, res_rounded, g0, g1 = call(
        residual_kernel,
        "residual",
        1.0,
        11,
        [vmem] * 3 + [hbm] * 8,
        [vmem] * 3 + [hbm] * 2,
        [data_half, f32_blocks, rounded, message, message],
        [two_messages, dma((16,)), dma((2,))],
    )(where, data_a, x_wide, partial, *second_buffers)
    g2, g3 = call(
        gradient_kernel,
        "gradient",
        0.5,
        8,
        [vmem] * 4,
        [hbm] * 2,
        [message, message],
        [two_messages, dma((2,))],
    )(where, data_a, data_b, residual, res_rounded)
    gradient = [g0, g1, g2, g3]
    returned = [from_home(gradient[k], k) for k in range(4)]
    change, sums = call(
        change_kernel,
        "change",
        1.0,
        12,
        [vmem] * 3 + [hbm] * 4,
        [vmem, smem],
        [f32_blocks, jax.ShapeDtypeStruct((2,), jnp.float32)],
        [wide, blocks, dma((12,))],
    )(where, data_a, data_b, residual, *gradient)

    sums = total(sums)
    step = -sums[0] / (sums[1] + 1e-06)

    new_primaries = jnp.zeros((2, MESSAGES, rows, width), jnp.bfloat16)
    new_residual = jnp.zeros((2, MESSAGES, rows, width), jnp.float32)
    updated = [(residual[k] + step * change[k]).astype(jnp.bfloat16) for k in range(4)]
    updated = [from_home(updated[k], k) for k in range(4)]
    for k in range(4):
        old = lax.dynamic_index_in_dim(prim_blocks, z ^ k, 1, keepdims=False)
        new = old.astype(jnp.float32) + step * returned[k].astype(jnp.float32)
        new_primaries = lax.dynamic_update_index_in_dim(
            new_primaries, new.astype(jnp.bfloat16), z ^ k, 1
        )
        new_residual = lax.dynamic_update_index_in_dim(
            new_residual, updated[k].astype(jnp.float32), z ^ k, 1
        )
    return new_primaries.reshape(data.shape), new_residual.reshape(data.shape)


def solution(mesh):
    shape = tuple(mesh.shape[name] for name in ("row", "col", "freq"))
    if shape == (2, 4, 4):
        fine = Mesh(np.asarray(mesh.devices).reshape(2, 2, 2, 2, 2), FINE)
        spec = P(None, ("twin", "lane"), "row", ("half", "pair"))
        local = whole_rows
    else:
        fine, spec, local = mesh, P(None, "freq", "row", "col"), blocked
    return jax.shard_map(
        local, mesh=fine, in_specs=(spec, spec), out_specs=(spec, spec), check_vma=False
    )
```

```python
import jax
import jax.numpy as jnp
import numpy as np
from jax import lax
from jax.experimental import pallas as pl
from jax.experimental.pallas import tpu as pltpu
from jax.sharding import Mesh
from jax.sharding import PartitionSpec as P

MIB = 1024 * 1024


def batched(left, right):
    return jnp.einsum("fik,fkj->fij", left, right, preferred_element_type=jnp.float32)


def complex_product(left, right):
    real = batched(left[0], right[0]) - batched(left[1], right[1])
    imag = batched(left[0], right[1]) + batched(left[1], right[0])
    return jnp.stack([real, imag])


def blocked_gradient(data_part, primary_part):
    src_rows = data_part.shape[2]
    columns = lax.all_gather(data_part, "row", axis=2, tiled=True)

    def add_block(piece):
        return complex_product(piece, columns)

    forward = add_block(lax.all_gather(primary_part, "col", axis=3, tiled=True))
    residual = data_part.astype(jnp.float32) - primary_part.astype(jnp.float32) + forward
    rounded = residual.astype(jnp.bfloat16)
    real = jnp.einsum("fjk,fik->jfi", columns[0], rounded[0], preferred_element_type=jnp.float32)
    real = real + jnp.einsum(
        "fjk,fik->jfi", columns[1], rounded[1], preferred_element_type=jnp.float32
    )
    imag = jnp.einsum("fjk,fik->jfi", columns[0], rounded[1], preferred_element_type=jnp.float32)
    imag = imag - jnp.einsum(
        "fjk,fik->jfi", columns[1], rounded[0], preferred_element_type=jnp.float32
    )
    summed = lax.psum_scatter(
        jnp.concatenate([real, imag], axis=2), "col", scatter_dimension=0, tiled=True
    )
    adjoint = jnp.stack([summed[:, :, :src_rows], summed[:, :, src_rows:]]).transpose(0, 2, 3, 1)
    gradient = (adjoint - residual).astype(jnp.bfloat16)
    moved = add_block(lax.all_gather(gradient, "col", axis=3, tiled=True))
    change = moved - gradient.astype(jnp.float32)
    return (residual, gradient, change)


def blocked(data, primaries):
    res, grad, chg = blocked_gradient(data, primaries)
    inner_local = jnp.sum(chg * res)
    energy_local = jnp.sum(chg * chg)
    inner, energy = lax.psum((inner_local, energy_local), ("row", "col", "freq"))
    step = -inner / (energy + 1e-06)
    updated_primaries = (primaries.astype(jnp.float32) + step * grad.astype(jnp.float32)).astype(
        jnp.bfloat16
    )
    updated_residual = res + step * chg
    return (updated_primaries, updated_residual)


FINE = ("row", "half", "pair", "twin", "lane")
MESSAGES = 4
GROUPS = ((0, 1), (2, 3))
OFFSETS = tuple((dx, dp) for dx in range(2) for dp in range(4))


def send_pairs(k):
    pairs = []
    for z in range(4):
        for f in range(4):
            twin, lane, part = f // 2, f % 2, z ^ k
            pairs.append((z * 4 + f, (lane * 2 + part // 2) * 4 + twin * 2 + part % 2))
    return pairs


COLUMN = ("half", "pair", "twin", "lane")


def to_home(blocks, z, k):
    piece = lax.dynamic_index_in_dim(blocks, z ^ k, 1, keepdims=False)
    return lax.ppermute(piece, COLUMN, send_pairs(k))


def from_home(piece, k):
    return lax.ppermute(piece, COLUMN, [(b, a) for a, b in send_pairs(k)])


def swap(value, axis):
    return lax.ppermute(value, axis, [(0, 1), (1, 0)])


def pinned(value):
    return pltpu.with_memory_space_constraint(value, pltpu.HBM)


def total(value):
    value = value + swap(value, "lane")
    for axes in (("row", "twin"), ("half", "pair")):
        across = lax.ppermute(value, axes, [(i, 3 - i) for i in range(4)])
        value = (value + swap(value, axes[1])) + (swap(value, axes[0]) + across)
    return value


def place_copies(group, buffers, where, data_v, sems, rows):
    row_index, part = where
    copies = [[] for _ in range(4)]
    for number, ((dx, dp), buffer) in enumerate(zip(OFFSETS, buffers)):
        start = ((row_index ^ dx) * 2 + (part ^ dp) % 2) * rows
        at = pl.ds(pl.multiple_of(start, rows), rows)
        for sub, k in enumerate(group):
            target = data_v.at[dp ^ k, :, at, :]
            copies[dp ^ k].append(
                pltpu.make_async_copy(buffer.at[sub], target, sems.at[2 * number + sub])
            )
    return copies


def message_copies(refs, part, wide_v, blocks_v, sems, rows, width):
    copies = []
    for k in range(4):
        z = part ^ k
        at = pl.ds(pl.multiple_of(z // 2 * width, width), width)
        for i in range(2):
            target = wide_v.at[z % 2, pl.ds(i * rows, rows), at]
            copies.append(pltpu.make_async_copy(refs[k].at[i], target, sems.at[3 * k + i]))
        copies.append(pltpu.make_async_copy(refs[k], blocks_v.at[k], sems.at[3 * k + 2]))
    return copies


def product(stacked, right, n, rows):
    one = jnp.dot(stacked, right[n, 0], preferred_element_type=jnp.float32)
    two = jnp.dot(stacked, right[n, 1], preferred_element_type=jnp.float32)
    return one[:rows] - two[rows:], one[rows:] + two[:rows]


def against(left, right):
    dims = (((1,), (1,)), ((), ()))
    return lax.dot_general(left, right, dims, preferred_element_type=jnp.float32)


def gradient_blocks(second, part, a_v, b_v, r_v, rb_v, g_v, g_outs, sems, rows, width):
    half = part // 2
    at = pl.ds(pl.multiple_of((half ^ second) * width, width), width)
    for odd in range(2):
        one = two = None
        for t in range(4):
            source = a_v if odd == t // 2 else b_v
            first_dot = against(rb_v[t], source[t, 0, at, :])
            second_dot = against(rb_v[t], source[t, 1, at, :])
            one = first_dot if one is None else one + first_dot
            two = second_dot if two is None else two + second_dot
        slot = half ^ odd ^ part % 2
        k = slot + 2 * second
        g_v[slot, 0] = (one[:rows] + two[rows:] - r_v[k, 0]).astype(jnp.bfloat16)
        g_v[slot, 1] = (one[rows:] - two[:rows] - r_v[k, 1]).astype(jnp.bfloat16)
    outs = [pltpu.make_async_copy(g_v.at[j], g_outs[j], sems.at[j]) for j in range(2)]
    for copy in outs:
        copy.start()
    for copy in outs:
        copy.wait()


def collect_kernel(rows, width, where_ref, *refs):
    a_in, x_refs, d_refs, refs = refs[:8], refs[8:12], refs[12:16], refs[16:]
    a_v, wide_v, f_v, x_v, d_v, sems, x_sems, d_sems = refs
    part = where_ref[1]
    copies = place_copies(GROUPS[0], a_in, (where_ref[0], part), a_v, sems, rows)
    x_copies = message_copies(x_refs, part, wide_v, x_v, x_sems, rows, width)
    for k in range(4):
        x_copies.append(pltpu.make_async_copy(d_refs[k], d_v.at[k], d_sems.at[k]))
    for copy in copies[0] + x_copies + copies[1]:
        copy.start()
    for copy in x_copies:
        copy.wait()
    for t in range(4):
        for copy in copies[t]:
            copy.wait()
        if t < 2:
            for copy in copies[t + 2]:
                copy.start()
        forward = product(wide_v[part // 2 ^ t // 2], a_v, t, rows)
        for i in range(2):
            own = d_v[t, i].astype(jnp.float32) - x_v[t, i].astype(jnp.float32)
            f_v[t, i] = own + forward[i]


def residual_kernel(rows, width, where_ref, a_v, wide_v, f_v, *refs):
    b_in, (b_v, r_v, rb_v, g0, g1, g_v, b_sems, out_sems) = refs[:8], refs[8:]
    where = (where_ref[0], where_ref[1])
    part = where[1]
    copies = place_copies(GROUPS[1], b_in, where, b_v, b_sems, rows)
    for copy in copies[0] + copies[1]:
        copy.start()
    for t in range(4):
        for copy in copies[t]:
            copy.wait()
        if t < 2:
            for copy in copies[t + 2]:
                copy.start()
        forward = product(wide_v[1 - (part // 2 ^ t // 2)], b_v, t, rows)
        for i in range(2):
            residual = f_v[t, i] + forward[i]
            r_v[t, i] = residual
            rb_v[t, i * rows : (i + 1) * rows, :] = residual.astype(jnp.bfloat16)
    gradient_blocks(0, part, a_v, b_v, r_v, rb_v, g_v, (g0, g1), out_sems, rows, width)


def gradient_kernel(rows, width, where_ref, a_v, b_v, r_v, rb_v, g2, g3, g_v, out_sems):
    part = where_ref[1]
    gradient_blocks(1, part, a_v, b_v, r_v, rb_v, g_v, (g2, g3), out_sems, rows, width)


def change_kernel(rows, width, where_ref, a_v, b_v, r_v, *refs):
    g_refs, (c_v, sums_out, wide_v, g_v, g_sems) = refs[:4], refs[4:]
    part = where_ref[1]
    g_copies = message_copies(g_refs, part, wide_v, g_v, g_sems, rows, width)
    for copy in g_copies:
        copy.start()
    for copy in g_copies:
        copy.wait()
    inner = jnp.zeros((rows, width), jnp.float32)
    energy = jnp.zeros((rows, width), jnp.float32)
    for t in range(4):
        pair = part // 2 ^ t // 2
        from_a = product(wide_v[pair], a_v, t, rows)
        from_b = product(wide_v[1 - pair], b_v, t, rows)
        for i in range(2):
            change = from_a[i] + from_b[i] - g_v[t, i].astype(jnp.float32)
            c_v[t, i] = change
            inner = inner + change * r_v[t, i]
            energy = energy + change * change
    sums_out[0] = jnp.sum(inner)
    sums_out[1] = jnp.sum(energy)


def whole_rows(data, primaries):
    z = lax.axis_index("half") * 2 + lax.axis_index("pair")
    part = lax.axis_index("pair") * 2 + lax.axis_index("lane")
    n_rows, width = data.shape[2], data.shape[3]
    rows = n_rows // MESSAGES
    where = jnp.stack([lax.axis_index("row"), part]).astype(jnp.int32)
    data_blocks = data.reshape(2, MESSAGES, rows, width)
    prim_blocks = primaries.reshape(2, MESSAGES, rows, width)

    arrived = [to_home(data_blocks, z, k) for k in range(MESSAGES)]
    held = []
    for group in GROUPS:
        own = jnp.stack([arrived[k] for k in group])
        pieces = {(0, 0): own, (0, 2): swap(own, "pair"), (1, 0): swap(own, "row")}
        pieces[1, 2] = swap(pieces[0, 2], "row")
        held.append(pieces)
    ready = [[arrived, held[0][1, 0]], [held[1][1, 0], held[0][0, 2]], [held[1][0, 2]], [held[1][0, 2]]]
    x_parts = []
    for k in range(MESSAGES):
        later, _ = lax.optimization_barrier((prim_blocks, ready[k]))
        x_parts.append(to_home(later, z, k))

    def complete(pieces, after):
        for at, value in list(pieces.items()):
            if at != (1, 2):
                value, _ = lax.optimization_barrier((value, after))
            pieces[at[0], at[1] ^ 1] = swap(value, "lane")
        return [pinned(pieces[at]) for at in OFFSETS]

    held[1][1, 2], _ = lax.optimization_barrier((held[1][1, 2], x_parts))
    first_buffers = complete(held[0], [held[0][1, 2], x_parts[1]])
    second_buffers = complete(held[1], first_buffers[3])

    hbm = pl.BlockSpec(memory_space=pltpu.HBM)
    vmem = pl.BlockSpec(memory_space=pltpu.VMEM)
    smem = pl.BlockSpec(memory_space=pltpu.SMEM)
    message = jax.ShapeDtypeStruct((2, rows, width), jnp.bfloat16)
    f32_blocks = pltpu.VMEM((4, 2, rows, width), jnp.float32)
    data_half = pltpu.VMEM((4, 2, 4 * rows, width), jnp.bfloat16)
    wide = pltpu.VMEM((2, 2 * rows, 2 * width), jnp.bfloat16)
    blocks = pltpu.VMEM((4, 2, rows, width), jnp.bfloat16)
    rounded = pltpu.VMEM((4, 2 * rows, width), jnp.bfloat16)
    two_messages = pltpu.VMEM((2, 2, rows, width), jnp.bfloat16)
    dma = pltpu.SemaphoreType.DMA
    one_product = 8 * rows * (4 * width) * (4 * width)

    def call(kernel, name, products, mib, in_specs, out_specs, out_shape, scratch):
        return pl.pallas_call(
            lambda *refs: kernel(rows, width, *refs),
            in_specs=[smem] + in_specs,
            out_specs=out_specs,
            out_shape=out_shape,
            scratch_shapes=scratch,
            compiler_params=pltpu.CompilerParams(vmem_limit_bytes=mib * MIB),
            cost_estimate=pl.CostEstimate(
                flops=int(products * one_product), transcendentals=0, bytes_accessed=1 << 24
            ),
            name=name,
        )

    data_a, x_wide, partial = call(
        collect_kernel,
        "collect",
        0.5,
        13,
        [hbm] * 16,
        [vmem] * 3,
        [data_half, wide, f32_blocks],
        [blocks, blocks, dma((16,)), dma((12,)), dma((4,))],
    )(where, *first_buffers, *map(pinned, x_parts), *map(pinned, arrived))
    data_b, residual, res_rounded, g0, g1 = call(
        residual_kernel,
        "residual",
        1.0,
        11,
        [vmem] * 3 + [hbm] * 8,
        [vmem] * 3 + [hbm] * 2,
        [data_half, f32_blocks, rounded, message, message],
        [two_messages, dma((16,)), dma((2,))],
    )(where, data_a, x_wide, partial, *second_buffers)
    g2, g3 = call(
        gradient_kernel,
        "gradient",
        0.5,
        8,
        [vmem] * 4,
        [hbm] * 2,
        [message, message],
        [two_messages, dma((2,))],
    )(where, data_a, data_b, residual, res_rounded)
    gradient = [g0, g1, g2, g3]
    returned = [from_home(gradient[k], k) for k in range(4)]
    change, sums = call(
        change_kernel,
        "change",
        1.0,
        12,
        [vmem] * 3 + [hbm] * 4,
        [vmem, smem],
        [f32_blocks, jax.ShapeDtypeStruct((2,), jnp.float32)],
        [wide, blocks, dma((12,))],
    )(where, data_a, data_b, residual, *gradient)

    sums = total(sums)
    step = -sums[0] / (sums[1] + 1e-06)

    new_primaries = jnp.zeros((2, MESSAGES, rows, width), jnp.bfloat16)
    new_residual = jnp.zeros((2, MESSAGES, rows, width), jnp.float32)
    updated = [(residual[k] + step * change[k]).astype(jnp.bfloat16) for k in range(4)]
    updated = [from_home(updated[k], k) for k in range(4)]
    for k in range(4):
        old = lax.dynamic_index_in_dim(prim_blocks, z ^ k, 1, keepdims=False)
        new = old.astype(jnp.float32) + step * returned[k].astype(jnp.float32)
        new_primaries = lax.dynamic_update_index_in_dim(
            new_primaries, new.astype(jnp.bfloat16), z ^ k, 1
        )
        new_residual = lax.dynamic_update_index_in_dim(
            new_residual, updated[k].astype(jnp.float32), z ^ k, 1
        )
    return new_primaries.reshape(data.shape), new_residual.reshape(data.shape)


def solution(mesh):
    shape = tuple(mesh.shape[name] for name in ("row", "col", "freq"))
    if shape == (2, 4, 4):
        fine = Mesh(np.asarray(mesh.devices).reshape(2, 2, 2, 2, 2), FINE)
        spec = P(None, ("twin", "lane"), "row", ("half", "pair"))
        local = whole_rows
    else:
        fine, spec, local = mesh, P(None, "freq", "row", "col"), blocked
    return jax.shard_map(
        local, mesh=fine, in_specs=(spec, spec), out_specs=(spec, spec), check_vma=False
    )
```
